32 devices in a mesh: layer: 8 (over y, x, core), lat: 4 (over z).
Axes of the slice: x: 2, y: 2, z: 4, core: 2. Of those that a mesh axis runs over, the one named last changes fastest.
Arguments:
- activations: bfloat16 [1536, 4096], P('layer', 'lat'), may hold values from -6 to 6
- w_enc: bfloat16 [1536, 8192], P('layer', 'lat'), may hold values from -0.15625 to 0.15625
- w_dec: bfloat16 [1536, 8192], P('layer', 'lat'), may hold values from -0.25 to 0.25
- b_enc: bfloat16 [8192], P('lat'), may hold values from -3 to 3
- b_dec: float32 [1536], P('layer'), may hold values from -3 to 3
- tile_ids: int32 [4, 4], replicated, may hold values from -1 to 63, as said below
Outputs:
- d_w_enc: bfloat16 [1536, 8192], P('layer', 'lat')
- d_w_dec: bfloat16 [1536, 8192], P('layer', 'lat')
- d_b_enc: float32 [8192], P('lat')
The draws below stay inside these ranges and needn't reach their ends.
Inputs may be any that keep to these rules, and one draw needn't show every extreme that they name: `tile_ids`: row b lists the tiles of block b: live ids first, then -1. Live ids of a row are distinct, and no two of them share an owner id // 16. Each row has at least half of 4 (rounded up) live slots; some row has 4. One owner is named in every row.
All inputs are finite; a program needn't handle non-finite values.
Results may differ from the reference program's by a relative error of at most 0.02.
The reference program's roundings to bfloat16 on the way count: a program that leaves them out, or rounds other values in their place, can miss the bound.
Values may be sent and summed in bfloat16 or wider, within the bound.
No kernel may reach another device: no remote copies, remote signals or barrier semaphores. Data moves between devices by JAX's collectives and lax.ppermute only.
A program may use at most 64 MiB of HBM per device.

```python
import math
import jax
import jax.numpy as jnp
from jax import lax

TILE = 128
ROWS = 1024
FEAT_DEV = 192
FEAT = 1536
GROUPS = 8
LAT = 8192
TILES_DEV = 16
TILES = 64
BLOCKS = 4
KMAX = 4
TOKENS = 4096


def draw_tile_ids(key, part):
    subkeys = jax.random.split(jax.random.fold_in(key, 7), 5)
    common = jax.random.randint(subkeys[0], (), 0, BLOCKS)
    lowest = (KMAX + 1) // 2
    counts = jax.random.randint(subkeys[1], (BLOCKS,), lowest, KMAX + 1)
    full_row = jax.random.randint(subkeys[2], (), 0, BLOCKS)
    counts = jnp.where(jnp.arange(BLOCKS) == full_row, KMAX, counts)
    scores = jax.random.randint(subkeys[3], (BLOCKS, BLOCKS), 0, 1 << 20) * BLOCKS + jnp.arange(BLOCKS)[None, :]
    scores = jnp.where(jnp.arange(BLOCKS)[None, :] == common, -1, scores)
    ranked = jnp.argsort(scores, axis=1)[:, :KMAX]
    within = jax.random.randint(subkeys[4], (BLOCKS, KMAX), 0, TILES_DEV)
    tile_list = ranked * TILES_DEV + within
    live_slot = jnp.arange(KMAX)[None, :] < counts[:, None]
    return jnp.where(live_slot, tile_list, -1).astype(jnp.int32)


def shard_levels(own_key, extent, shards, low, largest):
    level = 1.0
    for dim, shards_of in shards:
        heights = jax.random.uniform(jax.random.fold_in(jax.random.fold_in(own_key, 6), dim), (shards_of,), jnp.float32, low / len(shards), largest / len(shards))
        level = level * jnp.repeat(jnp.exp(heights), extent[dim] // shards_of).reshape((-1,) + (1,) * (len(extent) - 1 - dim))
    return level


def bell_draw(key, shape, scale, limit, cuts=(), kind=jnp.bfloat16):
    result = jax.random.normal(key, shape, jnp.float32) * scale
    if len(cuts) > 0:
        result = shard_levels(key, shape, cuts, -0.22, 0.18) * result
    return jnp.clip(result, min=-limit, max=limit).astype(kind)


def setup_inputs(seed: int = 0) -> dict:
    seeds = jax.random.split(jax.random.key(seed), 7)
    activations = bell_draw(seeds[0], (FEAT, TOKENS), 1.0, 6.0, ((0, 8), (1, 4)))
    w_enc = bell_draw(seeds[1], (FEAT, LAT), FEAT ** -0.5, 0.15625, ((0, 8), (1, 4)))
    w_dec = bell_draw(seeds[2], (FEAT, LAT), (KMAX * TILE) ** -0.5, 0.25, ((0, 8), (1, 4)))
    b_enc = bell_draw(seeds[3], (LAT,), 0.5, 3.0, ((0, 4),))
    b_dec = bell_draw(seeds[4], (FEAT,), 0.5, 3.0, ((0, 8),), jnp.float32)
    tile_ids = draw_tile_ids(jax.random.fold_in(seeds[6], 71), 0)
    return {"activations": activations, "w_enc": w_enc, "w_dec": w_dec, "b_enc": b_enc, "b_dec": b_dec, "tile_ids": tile_ids}


def reference(activations, w_enc, w_dec, b_enc, b_dec, tile_ids):
    enc_table = w_enc.reshape(FEAT, TILES, TILE)
    dec_table = w_dec.reshape(FEAT, TILES, TILE)
    bias_table = b_enc.reshape(TILES, TILE)

    def one_block(totals, block_id):
        enc_total, dec_total, bias_total = totals
        slot_ids = lax.dynamic_index_in_dim(tile_ids, block_id, 0, keepdims=False)
        live_slot = slot_ids >= 0
        safe_ids = jnp.where(live_slot, slot_ids, 0).astype(jnp.int32)
        live_float = live_slot.astype(jnp.float32)
        block_acts = lax.dynamic_slice_in_dim(activations, block_id * ROWS, ROWS, 1).astype(jnp.float32)
        enc_cols = jnp.take(enc_table, safe_ids, axis=1).astype(jnp.float32) * live_float[None, :, None]
        dec_cols = jnp.take(dec_table, safe_ids, axis=1).astype(jnp.float32) * live_float[None, :, None]
        bias_cols = jnp.take(bias_table, safe_ids, axis=0).astype(jnp.float32)
        act_groups = block_acts.reshape(GROUPS, FEAT_DEV, ROWS)
        enc_parts = jnp.einsum('gfr,gfkc->grkc', act_groups, enc_cols.reshape(GROUPS, FEAT_DEV, KMAX, TILE))
        enc_parts = lax.optimization_barrier(enc_parts.astype(jnp.bfloat16)).astype(jnp.float32)
        preact = lax.optimization_barrier(jnp.sum(enc_parts, axis=0)) + bias_cols[None]
        latent_codes = (jax.nn.relu(preact) * live_float[None, :, None]).astype(jnp.bfloat16)
        codes_wide = latent_codes.astype(jnp.float32)
        rebuilt = jnp.einsum('rkc,fkc->fr', codes_wide, dec_cols) + b_dec[:, None]
        grad_err = ((rebuilt - block_acts) / math.sqrt(ROWS)).astype(jnp.bfloat16)
        grad_wide = grad_err.astype(jnp.float32)
        dec_part = jnp.einsum('fr,rkc->fkc', grad_wide, codes_wide)
        dec_part = lax.optimization_barrier(dec_part.astype(jnp.bfloat16)).astype(jnp.float32)
        back_parts = jnp.einsum('gfr,gfkc->grkc', grad_wide.reshape(GROUPS, FEAT_DEV, ROWS), dec_cols.reshape(GROUPS, FEAT_DEV, KMAX, TILE))
        back_parts = lax.optimization_barrier(back_parts.astype(jnp.bfloat16)).astype(jnp.float32)
        grad_total = lax.optimization_barrier(jnp.sum(back_parts, axis=0))
        code_grad = (grad_total * (codes_wide > 0)).astype(jnp.bfloat16)
        grad_codes = code_grad.astype(jnp.float32)
        enc_part = jnp.einsum('fr,rkc->fkc', block_acts, grad_codes)
        enc_part = lax.optimization_barrier(enc_part.astype(jnp.bfloat16)).astype(jnp.float32)
        bias_part = lax.optimization_barrier(jnp.sum(grad_codes, axis=0))
        bias_part = lax.optimization_barrier(bias_part.astype(jnp.bfloat16)).astype(jnp.float32)
        enc_total = enc_total.at[:, safe_ids].add(enc_part)
        dec_total = dec_total.at[:, safe_ids].add(dec_part)
        bias_total = bias_total.at[safe_ids].add(bias_part)
        return ((enc_total, dec_total, bias_total), None)
    start = (jnp.zeros((FEAT, TILES, TILE), jnp.float32), jnp.zeros((FEAT, TILES, TILE), jnp.float32), jnp.zeros((TILES, TILE), jnp.float32))
    totals, _ = lax.scan(one_block, start, jnp.arange(BLOCKS, dtype=jnp.int32))
    enc_total, dec_total, bias_total = totals
    return (enc_total.reshape(FEAT, LAT).astype(jnp.bfloat16), dec_total.reshape(FEAT, LAT).astype(jnp.bfloat16), bias_total.reshape(LAT))
```

```python
import functools
import math

import jax
import jax.numpy as jnp
from jax import lax
from jax.experimental import pallas as pl
from jax.experimental.pallas import tpu as pltpu
from jax.sharding import PartitionSpec as P

TILE = 128
LANES = 256
EXTRA = 16
F32 = jnp.float32
BF16 = jnp.bfloat16


def vmem():
    return pl.BlockSpec(memory_space=pltpu.VMEM)


def smem():
    return pl.BlockSpec(memory_space=pltpu.SMEM)


def hbm():
    return pl.BlockSpec(memory_space=pl.ANY)


def dot(a, b, da, db):
    return lax.dot_general(a, b, (((da,), (db,)), ((), ())), preferred_element_type=F32)


def call(kernel, outs, ins, args, scratch=(), flops=10**8, moved=10**6):
    return pl.pallas_call(
        kernel,
        out_shape=outs,
        in_specs=ins,
        out_specs=jax.tree.map(lambda _: vmem(), outs),
        scratch_shapes=list(scratch),
        cost_estimate=pl.CostEstimate(flops=flops, bytes_accessed=moved, transcendentals=0),
    )(*args)


def wanted_tile(ids_ref, block, owner, tiles):
    found = jnp.int32(-1)
    for slot in range(ids_ref.shape[1]):
        tile = ids_ref[block, slot]
        base = owner * tiles
        here = (tile >= base) & (tile < base + tiles)
        found = jnp.where(here, tile - base, found)
    return found


def pack_kernel(owners, tiles, place_ref, ids_ref, acts_ref, enc_ref, dec_ref, bias_ref, *rest):
    enc_out, dec_out = rest[:owners], rest[owners : 2 * owners]
    act_out, sem = rest[2 * owners : -1], rest[-1]
    features = enc_ref.shape[0]
    me = place_ref[0]
    chip = place_ref[1]
    quarter = act_out[0].shape[1]
    copies = []
    starts = []
    for step in range(owners):
        block = jnp.bitwise_xor(me, step)
        tile = jnp.maximum(wanted_tile(ids_ref, block, me, tiles), 0)
        starts.append(pl.multiple_of(tile * TILE, TILE))
    for step in range(owners):
        copies.append(
            pltpu.make_async_copy(
                enc_ref.at[:, pl.ds(starts[step], TILE)], enc_out[step], sem.at[len(copies)]
            )
        )
    for step in range(len(act_out)):
        start = pl.multiple_of(jnp.bitwise_xor(chip, step) * quarter, quarter)
        copies.append(
            pltpu.make_async_copy(acts_ref.at[:, pl.ds(start, quarter)], act_out[step], sem.at[len(copies)])
        )
    for step in range(owners):
        copies.append(
            pltpu.make_async_copy(
                dec_ref.at[:, pl.ds(starts[step], TILE)],
                dec_out[step].at[pl.ds(0, features), :],
                sem.at[len(copies)],
            )
        )
    for copy in copies:
        copy.start()
    for step in range(owners):
        row = bias_ref[:, pl.ds(starts[step], TILE)]
        dec_out[step][pl.ds(features, EXTRA), :] = jnp.broadcast_to(row, (EXTRA, TILE))
    for copy in copies:
        copy.wait()


def preact_kernel(chips, *refs):
    enc, acts, out_ref = refs[:chips], refs[chips : 2 * chips], refs[2 * chips]
    total = None
    for step in range(chips):
        part = dot(enc[step][...], acts[step][...], 0, 0).astype(BF16).astype(F32)
        total = part if total is None else total + part
    out_ref[...] = total


def decode_kernel(chips, cores, scale, place_ref, mine_ref, other_ref, bias_ref, *refs):
    dec, acts, offset = refs[:chips], refs[chips : 2 * chips], refs[2 * chips : 3 * chips]
    codes_ref, parts = refs[3 * chips], refs[3 * chips + 1 : 3 * chips + 1 + cores]
    errs = refs[3 * chips + 1 + cores : -1]
    total_ref = refs[-1]
    bias = bias_ref[:, :1]
    live = bias_ref[:, 1:2]
    pre = mine_ref[...] + other_ref[...] + bias
    codes = (jnp.maximum(pre, 0.0) * live).astype(BF16)
    codes_ref[...] = codes
    total = None
    for step in range(chips):
        rebuilt = dot(dec[step][...], codes, 1, 0) + offset[step][:, :1]
        err = ((rebuilt - acts[step][...].astype(F32)) * scale).astype(BF16)
        errs[step][...] = err
        part = dot(dec[step][...], err, 0, 0).astype(BF16).astype(F32)
        total = part if total is None else total + part
    total_ref[...] = total
    half = parts[0].shape[0]
    for step, part_ref in enumerate(parts):
        start = jnp.bitwise_xor(place_ref[2], step) * half
        part_ref[...] = total_ref[pl.ds(pl.multiple_of(start, half), half), :]


def decgrad_kernel(chips, codes_ref, *refs):
    codes = codes_ref[...]
    for step in range(chips):
        refs[chips + step][...] = dot(refs[step][...], codes, 1, 1).astype(BF16)


def mask_kernel(place_ref, codes_ref, *refs):
    parts, out_ref = refs[:-1], refs[-1]
    half = out_ref.shape[0]
    start = pl.multiple_of(place_ref[2] * half, half)
    codes = codes_ref[pl.ds(start, half), :].astype(F32)
    total = sum(part[...] for part in parts)
    out_ref[...] = jnp.where(codes > 0, total, 0.0).astype(BF16)


def sum_kernel(chips, owners, *refs):
    total = None
    for step in range(chips):
        part = refs[step][...].astype(F32)
        total = part if total is None else total + part
    total = total.astype(BF16)
    for step in range(owners):
        refs[chips + step][...] = total[:, step * TILE : (step + 1) * TILE]


def encgrad_kernel(chips, cores, owners, place_ref, acts_ref, *refs):
    count = chips * cores
    pieces, outs, all_ref = refs[:count], refs[count:-1], refs[-1]
    half, quarter = pieces[0].shape
    for step in range(count):
        col = jnp.bitwise_xor(place_ref[1], step // cores) * quarter
        row = jnp.bitwise_xor(place_ref[2], step % cores) * half
        where = (pl.ds(pl.multiple_of(row, half), half), pl.ds(pl.multiple_of(col, quarter), quarter))
        all_ref[where] = pieces[step][...]
    features = acts_ref.shape[0]
    grads = all_ref[...]
    enc = dot(acts_ref[...], grads, 1, 1).astype(BF16)
    ones = jnp.ones((EXTRA, grads.shape[1]), BF16)
    bias = dot(ones, grads, 1, 1).astype(BF16)
    for step in range(owners):
        outs[step][pl.ds(0, features), :] = enc[:, step * TILE : (step + 1) * TILE]
        outs[step][pl.ds(features, EXTRA), :] = bias[:, step * TILE : (step + 1) * TILE]


def place_kernel(owners, tiles, with_bias, place_ref, ids_ref, *refs):
    got, out_ref = refs[:owners], refs[owners]
    features = out_ref.shape[0]
    me = place_ref[0]
    found = [wanted_tile(ids_ref, jnp.bitwise_xor(me, step), me, tiles) for step in range(owners)]
    out_ref[...] = jnp.zeros_like(out_ref)
    if with_bias:
        refs[owners + 1][...] = jnp.zeros_like(refs[owners + 1])
    for step in range(owners):
        tile = found[step]

        @pl.when(tile >= 0)
        def _():
            total = None
            for peer in range(owners):
                part = got[peer][...].astype(F32)
                part = jnp.where(found[peer] == tile, part, 0.0)
                total = part if total is None else total + part
            start = pl.multiple_of(tile * TILE, TILE)
            out_ref[:, pl.ds(start, TILE)] = total[:features].astype(BF16)
            if with_bias:
                refs[owners + 1][:, pl.ds(start, TILE)] = total[features : features + 8]


def local(activations, w_enc, w_dec, b_enc, b_dec, tile_ids):
    features, rows = activations.shape
    latents = w_enc.shape[1]
    layers = lax.axis_size("layer")
    owners = lax.axis_size("lat")
    chips = min(layers, rows // LANES)
    cores = layers // chips
    tiles = latents // TILE
    width = owners * TILE
    half = width // cores
    quarter = rows // chips
    me = lax.axis_index("lat")
    layer = lax.axis_index("layer")
    chip, core = layer // cores, layer % cores
    place = jnp.stack([me, chip, core]).astype(jnp.int32)

    def over_lat(x, step):
        return lax.ppermute(x, "lat", [(i, i ^ step) for i in range(owners)])

    def over_chips(x, step):
        return lax.ppermute(x, "layer", [(i, i ^ (step * cores)) for i in range(layers)])

    def over_core(x, step):
        return lax.ppermute(x, "layer", [(i, i ^ step) for i in range(layers)])

    def shape(*dims, kind=BF16):
        return jax.ShapeDtypeStruct(dims, kind)

    packed = call(
        functools.partial(pack_kernel, owners, tiles),
        [shape(features, TILE)] * owners
        + [shape(features + EXTRA, TILE)] * owners
        + [shape(features, quarter)] * chips,
        [smem(), smem(), hbm(), hbm(), hbm(), vmem()],
        (place, tile_ids, activations, w_enc, w_dec, b_enc.reshape(1, latents)),
        [pltpu.SemaphoreType.DMA((2 * owners + chips,))],
    )
    enc_tiles, dec_tiles, acts = packed[:owners], packed[owners : 2 * owners], packed[2 * owners :]
    enc_tiles = [enc_tiles[0]] + [over_lat(enc_tiles[s], s) for s in range(1, owners)]
    acts = [acts[0]] + [over_chips(acts[s], s) for s in range(1, chips)]
    enc_own = jnp.concatenate(enc_tiles, axis=1)
    enc_all = [enc_own] + [over_chips(enc_own, s) for s in range(1, chips)]
    dec_tiles = [dec_tiles[0]] + [over_lat(dec_tiles[s], s) for s in range(1, owners)]
    dec_own = jnp.concatenate([tile[:features] for tile in dec_tiles], axis=1)
    dec_all = [dec_own] + [over_chips(dec_own, s) for s in range(1, chips)]
    offsets = [b_dec] + [over_chips(b_dec, s) for s in range(1, chips)]
    offsets = [jnp.broadcast_to(x[:, None], (features, TILE)) for x in offsets]
    bias = jnp.concatenate([tile[features] for tile in dec_tiles]).astype(F32)
    my_list = lax.dynamic_index_in_dim(tile_ids, me, 0, keepdims=False)
    slot_owner = me ^ jnp.arange(owners)
    live = jnp.any((my_list[None, :] >= 0) & (my_list[None, :] // tiles == slot_owner[:, None]), axis=1)
    live = jnp.repeat(live.astype(F32), TILE)
    lane = lax.broadcasted_iota(jnp.int32, (width, TILE), 1)
    bias_live = jnp.where(lane == 0, bias[:, None], live[:, None])

    mine = call(
        functools.partial(preact_kernel, chips),
        shape(width, quarter, kind=F32),
        [vmem()] * (2 * chips),
        (*enc_all, *acts),
    )
    step = 1
    while 2 * step < cores:
        mine = mine + over_core(mine, step)
        step = 2 * step
    other = over_core(mine, step)
    out = call(
        functools.partial(decode_kernel, chips, cores, 1.0 / math.sqrt(rows)),
        [shape(width, quarter)] + [shape(half, quarter, kind=F32)] * cores + [shape(features, quarter)] * chips,
        [smem()] + [vmem()] * (3 + 3 * chips),
        (place, mine, other, bias_live, *dec_all, *acts, *offsets),
        [pltpu.VMEM((width, quarter), F32)],
    )
    codes, parts, errs = out[0], out[1 : 1 + cores], out[1 + cores :]
    parts = [parts[0]] + [over_core(parts[s], s) for s in range(1, cores)]
    dec_parts = call(
        functools.partial(decgrad_kernel, chips),
        [shape(features, width)] * chips,
        [vmem()] * (1 + chips),
        (codes, *errs),
    )
    code_grad = call(
        mask_kernel,
        shape(half, quarter),
        [smem()] + [vmem()] * (1 + cores),
        (place, codes, *parts),
    )
    grads = [code_grad] + [over_chips(code_grad, s) for s in range(1, chips)]
    grads = [[x] + [over_core(x, s) for s in range(1, cores)] for x in grads]
    dec_parts = [dec_parts[0]] + [over_chips(dec_parts[s], s) for s in range(1, chips)]
    dec_back = call(
        functools.partial(sum_kernel, chips, owners),
        [shape(features, TILE)] * owners,
        [vmem()] * chips,
        tuple(dec_parts),
    )
    dec_back = [dec_back[0]] + [over_lat(dec_back[s], s) for s in range(1, owners)]
    enc_back = call(
        functools.partial(encgrad_kernel, chips, cores, owners),
        [shape(features + EXTRA, TILE)] * owners,
        [smem()] + [vmem()] * (1 + layers),
        (place, activations, *sum(grads, [])),
        [pltpu.VMEM((width, rows), BF16)],
    )
    enc_back = [enc_back[0]] + [over_lat(enc_back[s], s) for s in range(1, owners)]
    d_w_dec = call(
        functools.partial(place_kernel, owners, tiles, False),
        shape(features, latents),
        [smem(), smem()] + [vmem()] * owners,
        (place, tile_ids, *dec_back),
    )
    d_w_enc, d_b_enc = call(
        functools.partial(place_kernel, owners, tiles, True),
        [shape(features, latents), shape(8, latents, kind=F32)],
        [smem(), smem()] + [vmem()] * owners,
        (place, tile_ids, *enc_back),
    )
    return (d_w_enc, d_w_dec, d_b_enc[0])


def solution(mesh):
    return jax.shard_map(
        local,
        mesh=mesh,
        in_specs=(
            P("layer", "lat"),
            P("layer", "lat"),
            P("layer", "lat"),
            P("lat"),
            P("layer"),
            P(),
        ),
        out_specs=(P("layer", "lat"), P("layer", "lat"), P("lat")),
        check_vma=False,
    )
```

```python
import functools
import math

import jax
import jax.numpy as jnp
from jax import lax
from jax.experimental import pallas as pl
from jax.experimental.pallas import tpu as pltpu
from jax.sharding import PartitionSpec as P

TILE = 128
PARTS = 4
EXTRA = 16
F32 = jnp.float32
BF16 = jnp.bfloat16


def vmem():
    return pl.BlockSpec(memory_space=pltpu.VMEM)


def smem():
    return pl.BlockSpec(memory_space=pltpu.SMEM)


def anywhere():
    return pl.BlockSpec(memory_space=pl.ANY)


def dot(a, b, da, db):
    return lax.dot_general(a, b, (((da,), (db,)), ((), ())), preferred_element_type=F32)


def call(kernel, outs, ins, args, out_specs=None, scratch=(), limit=8 << 20, alias=None):
    return pl.pallas_call(
        kernel,
        out_shape=outs,
        in_specs=ins,
        out_specs=jax.tree.map(lambda _: vmem(), outs) if out_specs is None else out_specs,
        scratch_shapes=list(scratch),
        input_output_aliases=alias or {},
        compiler_params=pltpu.CompilerParams(vmem_limit_bytes=limit),
        cost_estimate=pl.CostEstimate(flops=10**8, bytes_accessed=10**6, transcendentals=0),
    )(*args)


def shape(*dims, kind=BF16):
    return jax.ShapeDtypeStruct(dims, kind)


def place(parts):
    layer = lax.axis_index("layer")
    cores = lax.axis_size("layer") // parts
    return lax.axis_index("lat"), lax.div(layer, cores), lax.rem(layer, cores)


def xor(a, b):
    return jnp.bitwise_xor(a, b)


def lanes(index, size):
    return pl.ds(pl.multiple_of(index * size, size), size)


def wanted_tile(ids_ref, block, owner, tiles):
    found = jnp.int32(-1)
    base = owner * tiles
    for slot in range(ids_ref.shape[1]):
        tile = ids_ref[block, slot]
        here = (tile >= base) & (tile < base + tiles)
        found = jnp.where(here, tile - base, found)
    return found


def send_lanes(ids_ref, me, step, tiles):
    tile = wanted_tile(ids_ref, xor(me, step), me, tiles)
    return lanes(jnp.maximum(tile, 0), TILE)


def first_kernel(owners, tiles, parts, ids_ref, enc_ref, dec_ref, bias_ref, *rest):
    outs, sem = rest[:-1], rest[-1]
    features = enc_ref.shape[0]
    me, _, _ = place(parts)
    copies = []
    for step in range(1, owners):
        where = send_lanes(ids_ref, me, step, tiles)
        for index, source in enumerate((enc_ref, dec_ref)):
            target = outs[step - 1].at[pl.ds(index * features, features), :]
            copies.append(pltpu.make_async_copy(source.at[:, where], target, sem.at[len(copies)]))
    for copy in copies:
        copy.start()
    for step in range(1, owners):
        bias = bias_ref[:, send_lanes(ids_ref, me, step, tiles)]
        outs[step - 1][pl.ds(2 * features, EXTRA), :] = jnp.broadcast_to(bias, (EXTRA, TILE))
    for copy in copies:
        copy.wait()


def second_kernel(tiles, parts, ids_ref, acts_ref, enc_ref, dec_ref, bias_ref, offset_ref, *rest):
    messages, bias_out, sem = rest[:parts], rest[-2], rest[-1]
    features, rows = acts_ref.shape
    quarter = rows // parts
    me, part, _ = place(parts)
    inner = pl.ds(0, features)
    here = send_lanes(ids_ref, me, 0, tiles)
    copies = []
    for step in range(parts):
        out = messages[step]
        acts = acts_ref.at[:, lanes(xor(part, step), quarter)]
        start = 0
        for source in (acts, enc_ref.at[:, here], dec_ref.at[:, here]):
            size = source.shape[1]
            target = out.at[inner, pl.ds(start, size)]
            copies.append(pltpu.make_async_copy(source, target, sem.at[len(copies)]))
            start += size
    for copy in copies:
        copy.start()
    offset = offset_ref[...]
    high = offset.astype(BF16)
    rest_one = offset - high.astype(F32)
    middle = rest_one.astype(BF16)
    low = (rest_one - middle.astype(F32)).astype(BF16)
    row = lax.broadcasted_iota(jnp.int32, (EXTRA, features), 0)
    split = jnp.where(row == 0, high.astype(F32), 0.0)
    split = jnp.where(row == 1, middle.astype(F32), split)
    split = jnp.where(row == 2, low.astype(F32), split).astype(BF16)
    for step in range(parts):
        messages[step][pl.ds(features, EXTRA), :] = jnp.zeros((EXTRA, quarter + 2 * TILE), BF16)
        messages[step][pl.ds(features, EXTRA), pl.ds(0, features)] = split
    bias_out[...] = jnp.broadcast_to(bias_ref[:, here], (EXTRA, TILE))
    for copy in copies:
        copy.wait()


def join_kernel(owners, bias_ref, *refs):
    got, enc_out, dec_out, bias_out = refs[: owners - 1], refs[-3], refs[-2], refs[-1]
    features = enc_out.shape[0]
    bias_out[:, pl.ds(0, TILE)] = bias_ref[...]
    for step in range(owners - 1):
        enc_out[:, pl.ds(step * TILE, TILE)] = got[step][pl.ds(0, features), :]
        dec_out[:, pl.ds(step * TILE, TILE)] = got[step][pl.ds(features, features), :]
        bias_out[:, pl.ds((step + 1) * TILE, TILE)] = got[step][pl.ds(2 * features, EXTRA), :]


def zero_kernel(*refs):
    outs, hold, sem = refs[:-2], refs[-2], refs[-1]
    hold[...] = jnp.zeros_like(hold)
    width = hold.shape[1]
    copies = []
    for out in outs:
        for start in range(0, out.shape[1], width):
            target = out.at[:, pl.ds(start, width)]
            copies.append(pltpu.make_async_copy(hold, target, sem.at[len(copies)]))
    for copy in copies:
        copy.start()
    for copy in copies:
        copy.wait()


def preact_kernel(parts, *refs):
    messages, encs, out_ref = refs[:parts], refs[parts : 2 * parts], refs[-1]
    features = encs[0].shape[0]
    quarter = out_ref.shape[1]
    inner = pl.ds(0, features)
    one, two = None, None
    for step in range(parts):
        acts = messages[step][inner, pl.ds(0, quarter)]
        first = dot(messages[step][inner, pl.ds(quarter, TILE)], acts, 0, 0).astype(BF16).astype(F32)
        second = dot(encs[step][...], acts, 0, 0).astype(BF16).astype(F32)
        one = first if one is None else one + first
        two = second if two is None else two + second
    out_ref[pl.ds(0, TILE), :] = one
    out_ref[pl.ds(TILE, out_ref.shape[0] - TILE), :] = two


def codes_kernel(owners, tiles, parts, ids_ref, mine_ref, other_ref, bias_ref, out_ref):
    me, _, _ = place(parts)
    quarter = out_ref.shape[1]
    row = lax.broadcasted_iota(jnp.int32, (EXTRA, quarter), 0)
    pick = jnp.where(row == 0, 1.0, 0.0).astype(BF16)
    for step in range(owners):
        live = wanted_tile(ids_ref, me, xor(me, step), tiles) >= 0
        where = pl.ds(step * TILE, TILE)
        bias = dot(bias_ref[:, where], pick, 0, 0)
        pre = mine_ref[where, :] + other_ref[where, :] + bias
        out_ref[where, :] = jnp.where(live, jnp.maximum(pre, 0.0), 0.0).astype(BF16)


def decode_kernel(count, cores, parts, scale, first, last, codes_ref, *refs):
    refs = list(refs)
    before = None if first else refs.pop(0)
    messages, decs = refs[:count], refs[count : 2 * count]
    grads = refs[2 * count : 3 * count]
    outs = refs[3 * count :]
    features, width = grads[0].shape
    quarter = codes_ref.shape[1]
    inner = pl.ds(0, features)
    row = lax.broadcasted_iota(jnp.int32, (EXTRA, quarter), 0)
    pick = jnp.where(row < 3, 1.0, 0.0).astype(BF16)
    codes = codes_ref[...]
    one = None if first else before[pl.ds(0, TILE), :]
    two = None if first else before[pl.ds(TILE, width - TILE), :]
    for step in range(count):
        message, dec = messages[step], decs[step][...]
        acts = message[inner, pl.ds(0, quarter)].astype(F32)
        tile = message[inner, pl.ds(quarter + TILE, TILE)]
        offset = dot(message[pl.ds(features, EXTRA), pl.ds(0, features)], pick, 0, 0)
        rebuilt = dot(tile, codes[:TILE], 1, 0) + dot(dec, codes[TILE:], 1, 0) + offset
        err = ((rebuilt - acts) * scale).astype(BF16)
        grads[step][...] = dot(err, codes, 1, 1).astype(BF16)
        left = dot(tile, err, 0, 0).astype(BF16).astype(F32)
        right = dot(dec, err, 0, 0).astype(BF16).astype(F32)
        one = left if one is None else one + left
        two = right if two is None else two + right
    total = outs[-1]
    total[pl.ds(0, TILE), :] = one
    total[pl.ds(TILE, width - TILE), :] = two
    if last:
        _, _, core = place(parts)
        half = width // cores
        for step in range(cores):
            outs[step][...] = total[lanes(xor(core, step), half), :]


def mask_kernel(parts, codes_ref, *refs):
    sums, out_ref = refs[:-1], refs[-1]
    _, _, core = place(parts)
    codes = codes_ref[lanes(core, out_ref.shape[0]), :].astype(F32)
    total = sums[0][...]
    for other in sums[1:]:
        total = total + other[...]
    out_ref[...] = jnp.where(codes > 0, total, 0.0).astype(BF16)


def sum_kernel(parts, owners, *refs):
    total = None
    for step in range(parts):
        part = refs[step][...].astype(F32)
        total = part if total is None else total + part
    total = total.astype(BF16)
    for step in range(owners):
        refs[parts + step][...] = total[:, step * TILE : (step + 1) * TILE]


def encgrad_kernel(parts, cores, owners, *refs):
    acts, pieces = refs[:cores], refs[cores : cores + parts]
    outs, all_ref = refs[cores + parts : -1], refs[-1]
    quarter = pieces[0].shape[1]
    features = acts[0].shape[0]
    share = owners // cores
    _, part, _ = place(parts)
    for step in range(parts):
        all_ref[:, lanes(xor(part, step), quarter)] = pieces[step][...]
    grads = all_ref[...]
    bias = dot(jnp.ones((EXTRA, grads.shape[1]), BF16), grads, 1, 1).astype(BF16)
    for step in range(cores):
        back = dot(acts[step][...], grads, 1, 1).astype(BF16)
        for tile in range(share):
            where = slice(tile * TILE, (tile + 1) * TILE)
            outs[step * share + tile][pl.ds(0, features), :] = back[:, where]
            outs[step * share + tile][pl.ds(features, EXTRA), :] = bias[:, where]


def place_kernel(owners, cores, tiles, parts, crossed, ids_ref, zero_ref, *refs):
    got, out_ref = refs[:owners], refs[owners]
    hold, sem = refs[-2], refs[-1]
    features = out_ref.shape[0]
    me, _, core = place(parts)
    share = owners // cores
    found = []
    for step in range(owners):
        slot = xor(core, step // share) * share + step % share if crossed else step
        found.append(wanted_tile(ids_ref, xor(me, slot), me, tiles))
    if crossed:
        refs[owners + 1][...] = jnp.zeros_like(refs[owners + 1])
    fresh = []
    for step in range(owners):
        new = found[step] >= 0
        for peer in range(step):
            new = new & (found[peer] != found[step])
        fresh.append(new)

    def copy(step):
        where = lanes(jnp.maximum(found[step], 0), TILE)
        return pltpu.make_async_copy(hold.at[step], out_ref.at[:, where], sem.at[step])

    for step in range(owners):

        @pl.when(fresh[step])
        def _():
            total = got[step][...].astype(F32)
            for peer in range(step + 1, owners):
                total = total + jnp.where(
                    found[peer] == found[step], got[peer][...].astype(F32), 0.0
                )
            hold[step] = total[:features].astype(BF16)
            copy(step).start()
            if crossed:
                refs[owners + 1][:, lanes(found[step], TILE)] = total[features : features + 1]

    for step in range(owners):

        @pl.when(fresh[step])
        def _():
            copy(step).wait()


def sizes(mesh):
    owners, layers = mesh.shape["lat"], mesh.shape["layer"]
    parts = min(PARTS, layers)
    return owners, layers, parts, layers // parts


def local(owners, layers, parts, cores, activations, w_enc, w_dec, b_enc, b_dec, tile_ids):
    features, rows = activations.shape
    latents = w_enc.shape[1]
    tiles = latents // TILE
    width = owners * TILE
    half = width // cores
    quarter = rows // parts
    share = owners // cores

    def over_lat(x, step):
        return lax.ppermute(x, "lat", [(i, i ^ step) for i in range(owners)])

    def over_layer(x, step, stride):
        return lax.ppermute(x, "layer", [(i, i ^ (step * stride)) for i in range(layers)])

    def crossed(x, step):
        pairs = []
        for layer in range(layers):
            part, core = layer // cores, layer % cores
            goal = part * cores + (core ^ (step // share))
            for z in range(owners):
                owner = z ^ (core * share + step % share)
                pairs.append((layer * owners + z, goal * owners + owner))
        return lax.ppermute(x, ("layer", "lat"), pairs)

    def gather(x):
        return [x] + [over_layer(x, s, cores) for s in range(1, parts)]

    bias_line = b_enc.reshape(1, latents)
    moved = call(
        functools.partial(first_kernel, owners, tiles, parts),
        [shape(2 * features + EXTRA, TILE)] * (owners - 1),
        [smem(), anywhere(), anywhere(), vmem()],
        (tile_ids, w_enc, w_dec, bias_line),
        scratch=[pltpu.SemaphoreType.DMA((2 * (owners - 1),))],
    )
    second = call(
        functools.partial(second_kernel, tiles, parts),
        [shape(features + EXTRA, quarter + 2 * TILE)] * parts + [shape(EXTRA, TILE)],
        [smem(), anywhere(), anywhere(), anywhere(), vmem(), vmem()],
        (tile_ids, activations, w_enc, w_dec, bias_line, b_dec.reshape(1, features)),
        scratch=[pltpu.SemaphoreType.DMA((3 * parts,))],
    )
    messages, own_bias = second[:parts], second[-1]
    moved = [over_lat(x, s + 1) for s, x in enumerate(moved)]
    messages = [messages[0]] + [over_layer(messages[s], s, cores) for s in range(1, parts)]
    all_acts = [activations] + [over_layer(activations, s, 1) for s in range(1, cores)]
    enc_rest, dec_rest, bias_rows = call(
        functools.partial(join_kernel, owners),
        [shape(features, width - TILE)] * 2 + [shape(EXTRA, width)],
        [vmem()] * owners,
        (own_bias, *moved),
    )
    encs = gather(enc_rest)
    decs = gather(dec_rest)

    mine = call(
        functools.partial(preact_kernel, parts),
        shape(width, quarter, kind=F32),
        [vmem()] * (2 * parts),
        (*messages, *encs),
    )
    step = 1
    while 2 * step < cores:
        mine = mine + over_layer(mine, step, 1)
        step = 2 * step
    other = over_layer(mine, step, 1)
    codes = call(
        functools.partial(codes_kernel, owners, tiles, parts),
        shape(width, quarter),
        [smem()] + [vmem()] * 3,
        (tile_ids, mine, other, bias_rows),
    )
    groups = [[0], list(range(1, parts - 1)), [parts - 1]]
    total, sent = None, []
    for index, group in enumerate(groups):
        first, last = index == 0, index == len(groups) - 1
        outs = [shape(features, width)] * len(group)
        if last:
            outs += [shape(half, quarter, kind=F32)] * cores
        outs += [shape(width, quarter, kind=F32)]
        args = [codes] + ([] if first else [total])
        args += [messages[s] for s in group] + [decs[s] for s in group]
        out = call(
            functools.partial(
                decode_kernel, len(group), cores, parts, 1.0 / math.sqrt(rows), first, last
            ),
            outs,
            [vmem()] * len(args),
            tuple(args),
        )
        sent += out[: len(group)]
        total = out[-1]
        sums = out[len(group) : -1]
    sums = [sums[0]] + [over_layer(sums[s], s, 1) for s in range(1, cores)]
    grad = call(
        functools.partial(mask_kernel, parts),
        shape(half, quarter),
        [vmem()] * (1 + cores),
        (codes, *sums),
    )
    grads = gather(grad)
    sent = [sent[0]] + [over_layer(sent[s], s, cores) for s in range(1, parts)]
    dec_back = call(
        functools.partial(sum_kernel, parts, owners),
        [shape(features, TILE)] * owners,
        [vmem()] * parts,
        tuple(sent),
    )
    dec_back = [dec_back[0]] + [over_lat(dec_back[s], s) for s in range(1, owners)]
    enc_back = call(
        functools.partial(encgrad_kernel, parts, cores, owners),
        [shape(features + EXTRA, TILE)] * owners,
        [vmem()] * (cores + parts),
        (*all_acts, *grads),
        scratch=[pltpu.VMEM((half, rows), BF16)],
    )
    enc_back = [crossed(x, s) for s, x in enumerate(enc_back)]
    zeros = call(
        zero_kernel,
        [shape(features, latents)] * 2,
        [],
        (),
        out_specs=[anywhere()] * 2,
        scratch=[
            pltpu.VMEM((features, 2 * TILE), BF16),
            pltpu.SemaphoreType.DMA((latents // TILE,)),
        ],
    )

    def put(cross, pieces, zero):
        outs = [shape(features, latents)] + ([shape(1, latents, kind=F32)] if cross else [])
        return call(
            functools.partial(place_kernel, owners, cores, tiles, parts, cross),
            outs,
            [smem(), anywhere()] + [vmem()] * owners,
            (tile_ids, zero, *pieces),
            out_specs=[anywhere()] + ([vmem()] if cross else []),
            scratch=[pltpu.VMEM((owners, features, TILE), BF16), pltpu.SemaphoreType.DMA((owners,))],
            alias={1: 0},
        )

    (d_w_dec,) = put(False, dec_back, zeros[0])
    d_w_enc, d_b_enc = put(True, enc_back, zeros[1])
    return (d_w_enc, d_w_dec, d_b_enc.reshape(latents))


def solution(mesh):
    owners, layers, parts, cores = sizes(mesh)

    def body(*args):
        return local(owners, layers, parts, cores, *args)

    return jax.shard_map(
        body,
        mesh=mesh,
        in_specs=(
            P("layer", "lat"),
            P("layer", "lat"),
            P("layer", "lat"),
            P("lat"),
            P("layer"),
            P(),
        ),
        out_specs=(P("layer", "lat"), P("layer", "lat"), P("lat")),
        check_vma=False,
    )
```

```python
import functools
import math

import jax
import jax.numpy as jnp
from jax import lax
from jax.experimental import pallas as pl
from jax.experimental.pallas import tpu as pltpu
from jax.sharding import PartitionSpec as P

TILE = 128
PARTS = 4
EXTRA = 16
F32 = jnp.float32
BF16 = jnp.bfloat16


def vmem():
    return pl.BlockSpec(memory_space=pltpu.VMEM)


def smem():
    return pl.BlockSpec(memory_space=pltpu.SMEM)


def anywhere():
    return pl.BlockSpec(memory_space=pl.ANY)


def in_hbm(x):
    return pltpu.with_memory_space_constraint(x, pltpu.HBM)


def dot(a, b, da, db):
    return lax.dot_general(a, b, (((da,), (db,)), ((), ())), preferred_element_type=F32)


def call(kernel, outs, ins, args, out_specs=None, scratch=(), limit=8 << 20, alias=None):
    return pl.pallas_call(
        kernel,
        out_shape=outs,
        in_specs=ins,
        out_specs=jax.tree.map(lambda _: vmem(), outs) if out_specs is None else out_specs,
        scratch_shapes=list(scratch),
        input_output_aliases=alias or {},
        compiler_params=pltpu.CompilerParams(vmem_limit_bytes=limit),
        cost_estimate=pl.CostEstimate(flops=10**8, bytes_accessed=10**6, transcendentals=0),
    )(*args)


def shape(*dims, kind=BF16):
    return jax.ShapeDtypeStruct(dims, kind)


def place(parts):
    layer = lax.axis_index("layer")
    cores = lax.axis_size("layer") // parts
    return lax.axis_index("lat"), lax.div(layer, cores), lax.rem(layer, cores)


def xor(a, b):
    return jnp.bitwise_xor(a, b)


def lanes(index, size):
    return pl.ds(pl.multiple_of(index * size, size), size)


def wanted_tile(ids_ref, block, owner, tiles):
    found = jnp.int32(-1)
    base = owner * tiles
    for slot in range(ids_ref.shape[1]):
        tile = ids_ref[block, slot]
        here = (tile >= base) & (tile < base + tiles)
        found = jnp.where(here, tile - base, found)
    return found


def send_lanes(ids_ref, me, step, tiles):
    tile = wanted_tile(ids_ref, xor(me, step), me, tiles)
    return lanes(jnp.maximum(tile, 0), TILE)


def bias_rows(ids_ref, bias_ref, me, step):
    tiles = bias_ref.shape[0]
    tile = wanted_tile(ids_ref, xor(me, step), me, tiles)
    row = lax.broadcasted_iota(jnp.int32, bias_ref.shape, 0)
    picked = jnp.where(row == tile, bias_ref[...].astype(F32), 0.0)
    line = jnp.sum(picked, axis=0, keepdims=True)
    live = jnp.where(tile >= 0, 1.0, 0.0)
    row = lax.broadcasted_iota(jnp.int32, (EXTRA, TILE), 0)
    return jnp.where(row == 0, line, live).astype(BF16)


def pack_kernel(owners, tiles, parts, ids_ref, acts_ref, enc_ref, dec_ref, bias_ref, offset_ref, *rest):
    moved, messages, bias_out, sem = rest[: owners - 1], rest[owners - 1 : -2], rest[-2], rest[-1]
    features, rows = acts_ref.shape
    quarter = rows // parts
    me, part, _ = place(parts)
    inner = pl.ds(0, features)
    pairs = []
    for step in range(1, owners):
        where = send_lanes(ids_ref, me, step, tiles)
        for index, source in enumerate((enc_ref, dec_ref)):
            target = moved[step - 1].at[pl.ds(index * features, features), :]
            pairs.append((source.at[:, where], target))
    here = send_lanes(ids_ref, me, 0, tiles)
    for step in range(parts):
        acts = acts_ref.at[:, lanes(xor(part, step), quarter)]
        start = 0
        for source in (acts, enc_ref.at[:, here], dec_ref.at[:, here]):
            size = source.shape[1]
            pairs.append((source, messages[step].at[inner, pl.ds(start, size)]))
            start += size
    copies = [pltpu.make_async_copy(a, b, sem.at[i]) for i, (a, b) in enumerate(pairs)]
    for copy in copies:
        copy.start()
    offset = offset_ref[...]
    high = offset.astype(BF16)
    rest_one = offset - high.astype(F32)
    middle = rest_one.astype(BF16)
    low = (rest_one - middle.astype(F32)).astype(BF16)
    row = lax.broadcasted_iota(jnp.int32, (EXTRA, features), 0)
    split = jnp.where(row == 0, high.astype(F32), 0.0)
    split = jnp.where(row == 1, middle.astype(F32), split)
    split = jnp.where(row == 2, low.astype(F32), split).astype(BF16)
    for step in range(parts):
        messages[step][pl.ds(features, EXTRA), :] = jnp.zeros((EXTRA, quarter + 2 * TILE), BF16)
        messages[step][pl.ds(features, EXTRA), pl.ds(0, features)] = split
    for step in range(1, owners):
        moved[step - 1][pl.ds(2 * features, EXTRA), :] = bias_rows(ids_ref, bias_ref, me, step)
    bias_out[...] = bias_rows(ids_ref, bias_ref, me, 0)
    for copy in copies:
        copy.wait()


def join_kernel(owners, bias_ref, *refs):
    got, enc_out, dec_out, bias_out = refs[: owners - 1], refs[-3], refs[-2], refs[-1]
    features = enc_out.shape[0]
    bias_out[:, pl.ds(0, TILE)] = bias_ref[...]
    for step in range(owners - 1):
        enc_out[:, pl.ds(step * TILE, TILE)] = got[step][pl.ds(0, features), :]
        dec_out[:, pl.ds(step * TILE, TILE)] = got[step][pl.ds(features, features), :]
        bias_out[:, pl.ds((step + 1) * TILE, TILE)] = got[step][pl.ds(2 * features, EXTRA), :]


def zero_kernel(*refs):
    outs, hold, sem = refs[:-2], refs[-2], refs[-1]
    hold[...] = jnp.zeros_like(hold)
    width = hold.shape[1]
    copies = []
    for out in outs:
        for start in range(0, out.shape[1], width):
            target = out.at[:, pl.ds(start, width)]
            copies.append(pltpu.make_async_copy(hold, target, sem.at[len(copies)]))
    for copy in copies:
        copy.start()
    for copy in copies:
        copy.wait()


def preact_kernel(parts, *refs):
    messages, encs, out_ref = refs[:parts], refs[parts : 2 * parts], refs[-1]
    features = encs[0].shape[0]
    quarter = out_ref.shape[1]
    inner = pl.ds(0, features)
    one, two = None, None
    for step in range(parts):
        acts = messages[step][inner, pl.ds(0, quarter)]
        first = dot(messages[step][inner, pl.ds(quarter, TILE)], acts, 0, 0).astype(BF16).astype(F32)
        second = dot(encs[step][...], acts, 0, 0).astype(BF16).astype(F32)
        one = first if one is None else one + first
        two = second if two is None else two + second
    out_ref[pl.ds(0, TILE), :] = one
    out_ref[pl.ds(TILE, out_ref.shape[0] - TILE), :] = two


def codes_of(mine_ref, other_ref, bias_ref):
    quarter = mine_ref.shape[1]
    row = lax.broadcasted_iota(jnp.int32, (EXTRA, quarter), 0)
    bias = dot(bias_ref[...], jnp.where(row == 0, 1.0, 0.0).astype(BF16), 0, 0)
    live = dot(bias_ref[...], jnp.where(row == 1, 1.0, 0.0).astype(BF16), 0, 0)
    pre = mine_ref[...] + other_ref[...] + bias
    return (jnp.maximum(pre, 0.0) * live).astype(BF16)


def decode_kernel(count, cores, parts, scale, first, last, *refs):
    refs = list(refs)
    if first:
        sources = [refs.pop(0) for _ in range(3)]
        codes_ref = refs.pop(2 * count)
        codes_ref[...] = codes_of(*sources)
        before = None
    else:
        codes_ref, before = refs.pop(0), refs.pop(0)
    messages, decs = refs[:count], refs[count : 2 * count]
    grads = refs[2 * count : 3 * count]
    outs = refs[3 * count :]
    features, width = grads[0].shape
    quarter = codes_ref.shape[1]
    inner = pl.ds(0, features)
    row = lax.broadcasted_iota(jnp.int32, (EXTRA, quarter), 0)
    pick = jnp.where(row < 3, 1.0, 0.0).astype(BF16)
    codes = codes_ref[...]
    one = None if first else before[pl.ds(0, TILE), :]
    two = None if first else before[pl.ds(TILE, width - TILE), :]
    for step in range(count):
        message, dec = messages[step], decs[step][...]
        acts = message[inner, pl.ds(0, quarter)].astype(F32)
        tile = message[inner, pl.ds(quarter + TILE, TILE)]
        offset = dot(message[pl.ds(features, EXTRA), pl.ds(0, features)], pick, 0, 0)
        rebuilt = dot(tile, codes[:TILE], 1, 0) + dot(dec, codes[TILE:], 1, 0) + offset
        err = ((rebuilt - acts) * scale).astype(BF16)
        grads[step][...] = dot(err, codes, 1, 1).astype(BF16)
        left = dot(tile, err, 0, 0).astype(BF16).astype(F32)
        right = dot(dec, err, 0, 0).astype(BF16).astype(F32)
        one = left if one is None else one + left
        two = right if two is None else two + right
    if last:
        _, _, core = place(parts)
        half = width // cores
        hold = outs[-1]
        for block in range(cores):
            start, stop = block * half, (block + 1) * half
            if start == 0:
                hold[xor(core, block), pl.ds(0, TILE), :] = one
                hold[xor(core, block), pl.ds(TILE, half - TILE), :] = two[: half - TILE]
            else:
                hold[xor(core, block)] = two[start - TILE : stop - TILE]
        for step in range(cores):
            outs[step][...] = hold[step]
    else:
        total = outs[-1]
        total[pl.ds(0, TILE), :] = one
        total[pl.ds(TILE, width - TILE), :] = two


def mask_kernel(parts, codes_ref, *refs):
    sums, out_ref = refs[:-1], refs[-1]
    _, _, core = place(parts)
    codes = codes_ref[lanes(core, out_ref.shape[0]), :].astype(F32)
    total = sums[0][...]
    for other in sums[1:]:
        total = total + other[...]
    out_ref[...] = jnp.where(codes > 0, total, 0.0).astype(BF16)


def sum_kernel(parts, owners, *refs):
    total = None
    for step in range(parts):
        part = refs[step][...].astype(F32)
        total = part if total is None else total + part
    total = total.astype(BF16)
    for step in range(owners):
        refs[parts + step][...] = total[:, step * TILE : (step + 1) * TILE]


def encgrad_kernel(parts, cores, owners, *refs):
    acts, pieces = refs[:cores], refs[cores : cores + parts]
    outs, all_ref = refs[cores + parts : -1], refs[-1]
    quarter = pieces[0].shape[1]
    features = acts[0].shape[0]
    share = owners // cores
    _, part, _ = place(parts)
    for step in range(parts):
        all_ref[:, lanes(xor(part, step), quarter)] = pieces[step][...]
    grads = all_ref[...]
    bias = dot(jnp.ones((EXTRA, grads.shape[1]), BF16), grads, 1, 1).astype(BF16)
    for step in range(cores):
        back = dot(acts[step][...], grads, 1, 1).astype(BF16)
        for tile in range(share):
            where = slice(tile * TILE, (tile + 1) * TILE)
            outs[step * share + tile][pl.ds(0, features), :] = back[:, where]
            outs[step * share + tile][pl.ds(features, EXTRA), :] = bias[:, where]


def place_kernel(owners, cores, tiles, parts, crossed, ids_ref, zero_ref, *refs):
    got, out_ref = refs[:owners], refs[owners]
    hold, sem = refs[-2], refs[-1]
    features = out_ref.shape[0]
    me, _, core = place(parts)
    share = owners // cores
    found = []
    for step in range(owners):
        slot = xor(core, step // share) * share + step % share if crossed else step
        found.append(wanted_tile(ids_ref, xor(me, slot), me, tiles))
    if crossed:
        bias_out, bias_hold, bias_sem = refs[owners + 1], refs[-4], refs[-3]
        bias_hold[...] = jnp.zeros_like(bias_hold)
        bias_copy = pltpu.make_async_copy(bias_hold, bias_out, bias_sem)
    fresh = []
    for step in range(owners):
        new = found[step] >= 0
        for peer in range(step):
            new = new & (found[peer] != found[step])
        fresh.append(new)

    def copy(step, source):
        where = lanes(jnp.maximum(found[step], 0), TILE)
        return pltpu.make_async_copy(source, out_ref.at[:, where], sem.at[step])

    for step in range(owners):
        again = jnp.bool_(False)
        for peer in range(step + 1, owners):
            again = again | (found[peer] == found[step])

        @pl.when(fresh[step] & jnp.logical_not(again))
        def _():
            copy(step, got[step].at[pl.ds(0, features), :]).start()

        @pl.when(fresh[step] & again)
        def _():
            total = got[step][pl.ds(0, features), :].astype(F32)
            for peer in range(step + 1, owners):
                same = got[peer][pl.ds(0, features), :].astype(F32)
                total = total + jnp.where(found[peer] == found[step], same, 0.0)
            hold[step] = total.astype(BF16)
            copy(step, hold.at[step]).start()

        if crossed:

            @pl.when(fresh[step])
            def _():
                total = got[step][pl.ds(features, EXTRA), :].astype(F32)
                for peer in range(step + 1, owners):
                    same = got[peer][pl.ds(features, EXTRA), :].astype(F32)
                    total = total + jnp.where(found[peer] == found[step], same, 0.0)
                bias_hold[:, lanes(found[step], TILE)] = total[:1]

    if crossed:
        bias_copy.start()
    for step in range(owners):

        @pl.when(fresh[step])
        def _():
            copy(step, hold.at[step]).wait()

    if crossed:
        bias_copy.wait()


def sizes(mesh):
    owners, layers = mesh.shape["lat"], mesh.shape["layer"]
    parts = min(PARTS, layers)
    return owners, layers, parts, layers // parts


def local(owners, layers, parts, cores, activations, w_enc, w_dec, b_enc, b_dec, tile_ids):
    features, rows = activations.shape
    latents = w_enc.shape[1]
    tiles = latents // TILE
    width = owners * TILE
    half = width // cores
    quarter = rows // parts
    share = owners // cores

    def over_lat(x, step):
        return lax.ppermute(x, "lat", [(i, i ^ step) for i in range(owners)])

    def over_layer(x, step, stride):
        return lax.ppermute(x, "layer", [(i, i ^ (step * stride)) for i in range(layers)])

    def crossed(x, step):
        pairs = []
        for layer in range(layers):
            part, core = layer // cores, layer % cores
            goal = part * cores + (core ^ (step // share))
            for z in range(owners):
                owner = z ^ (core * share + step % share)
                pairs.append((layer * owners + z, goal * owners + owner))
        return lax.ppermute(x, ("layer", "lat"), pairs)

    def gather(x):
        return [x] + [over_layer(x, s, cores) for s in range(1, parts)]

    bias_line = b_enc.reshape(tiles, TILE)
    packed = call(
        functools.partial(pack_kernel, owners, tiles, parts),
        [shape(2 * features + EXTRA, TILE)] * (owners - 1)
        + [shape(features + EXTRA, quarter + 2 * TILE)] * parts
        + [shape(EXTRA, TILE)],
        [smem(), anywhere(), anywhere(), anywhere(), vmem(), vmem()],
        (
            in_hbm(tile_ids),
            in_hbm(activations),
            in_hbm(w_enc),
            in_hbm(w_dec),
            in_hbm(bias_line),
            in_hbm(b_dec.reshape(1, features)),
        ),
        scratch=[pltpu.SemaphoreType.DMA((3 * parts + 2 * (owners - 1),))],
    )
    moved, messages, own_bias = packed[: owners - 1], packed[owners - 1 : -1], packed[-1]
    moved = [over_lat(x, s + 1) for s, x in enumerate(moved)]
    messages = [messages[0]] + [over_layer(messages[s], s, cores) for s in range(1, parts)]
    all_acts = [activations] + [over_layer(activations, s, 1) for s in range(1, cores)]
    enc_rest, dec_rest, bias_rows = call(
        functools.partial(join_kernel, owners),
        [shape(features, width - TILE)] * 2 + [shape(EXTRA, width)],
        [vmem()] * owners,
        (own_bias, *moved),
    )
    encs = gather(enc_rest)
    decs = gather(dec_rest)

    mine = call(
        functools.partial(preact_kernel, parts),
        shape(width, quarter, kind=F32),
        [vmem()] * (2 * parts),
        (*messages, *encs),
    )
    step = 1
    while 2 * step < cores:
        mine = mine + over_layer(mine, step, 1)
        step = 2 * step
    other = over_layer(mine, step, 1)
    groups = [[0], list(range(1, parts - 1)), [parts - 1]]
    total, sent = None, []
    for index, group in enumerate(groups):
        first, last = index == 0, index == len(groups) - 1
        outs = [shape(width, quarter)] if first else []
        outs += [shape(features, width)] * len(group)
        scratch = [pltpu.VMEM((cores, half, quarter), F32)] if last else []
        if last:
            outs += [shape(half, quarter, kind=F32)] * cores
        else:
            outs += [shape(width, quarter, kind=F32)]
        args = [mine, other, bias_rows] if first else [codes, total]
        args += [messages[s] for s in group] + [decs[s] for s in group]
        out = call(
            functools.partial(
                decode_kernel, len(group), cores, parts, 1.0 / math.sqrt(rows), first, last
            ),
            outs,
            [vmem()] * len(args),
            tuple(args),
            scratch=scratch,
        )
        if first:
            codes, out = out[0], out[1:]
        sent += out[: len(group)]
        total = out[-1]
        sums = out[len(group) :]
    sums = [sums[0]] + [over_layer(sums[s], s, 1) for s in range(1, cores)]
    grad = call(
        functools.partial(mask_kernel, parts),
        shape(half, quarter),
        [vmem()] * (1 + cores),
        (codes, *sums),
    )
    grads = gather(grad)
    sent = [sent[0]] + [over_layer(sent[s], s, cores) for s in range(1, parts)]
    dec_back = call(
        functools.partial(sum_kernel, parts, owners),
        [shape(features, TILE)] * owners,
        [vmem()] * parts,
        tuple(sent),
    )
    dec_back = [dec_back[0]] + [over_lat(dec_back[s], s) for s in range(1, owners)]
    enc_back = call(
        functools.partial(encgrad_kernel, parts, cores, owners),
        [shape(features + EXTRA, TILE)] * owners,
        [vmem()] * (cores + parts),
        (*all_acts, *grads),
        scratch=[pltpu.VMEM((half, rows), BF16)],
    )
    enc_back = [crossed(x, s) for s, x in enumerate(enc_back)]
    zeros = call(
        zero_kernel,
        [shape(features, latents)] * 2,
        [],
        (),
        out_specs=[anywhere()] * 2,
        scratch=[
            pltpu.VMEM((features, 2 * TILE), BF16),
            pltpu.SemaphoreType.DMA((latents // TILE,)),
        ],
    )

    def put(cross, pieces, zero):
        outs = [shape(features, latents)] + ([shape(1, latents, kind=F32)] if cross else [])
        return call(
            functools.partial(place_kernel, owners, cores, tiles, parts, cross),
            outs,
            [smem(), anywhere()] + [vmem()] * owners,
            (tile_ids, zero, *pieces),
            out_specs=[anywhere()] * len(outs),
            scratch=([pltpu.VMEM((1, latents), F32), pltpu.SemaphoreType.DMA] if cross else [])
            + [pltpu.VMEM((owners, features, TILE), BF16), pltpu.SemaphoreType.DMA((owners,))],
            alias={1: 0},
        )

    (d_w_dec,) = put(False, dec_back, zeros[0])
    d_w_enc, d_b_enc = put(True, enc_back, zeros[1])
    return (d_w_enc, d_w_dec, d_b_enc.reshape(latents))


def solution(mesh):
    owners, layers, parts, cores = sizes(mesh)

    def body(*args):
        return local(owners, layers, parts, cores, *args)

    return jax.shard_map(
        body,
        mesh=mesh,
        in_specs=(
            P("layer", "lat"),
            P("layer", "lat"),
            P("layer", "lat"),
            P("lat"),
            P("layer"),
            P(),
        ),
        out_specs=(P("layer", "lat"), P("layer", "lat"), P("lat")),
        check_vma=False,
    )
```

```python
import functools
import math

import jax
import jax.numpy as jnp
from jax import lax
from jax.experimental import pallas as pl
from jax.experimental.pallas import tpu as pltpu
from jax.sharding import PartitionSpec as P

TILE = 128
PARTS = 4
EXTRA = 8
F32 = jnp.float32
BF16 = jnp.bfloat16


def vmem():
    return pl.BlockSpec(memory_space=pltpu.VMEM)


def smem():
    return pl.BlockSpec(memory_space=pltpu.SMEM)


def anywhere():
    return pl.BlockSpec(memory_space=pl.ANY)


def in_hbm(x):
    return pltpu.with_memory_space_constraint(x, pltpu.HBM)


def dot(a, b, da, db):
    return lax.dot_general(a, b, (((da,), (db,)), ((), ())), preferred_element_type=F32)


def call(kernel, outs, ins, args, out_specs=None, scratch=(), limit=8 << 20, alias=None):
    return pl.pallas_call(
        kernel,
        out_shape=outs,
        in_specs=ins,
        out_specs=jax.tree.map(lambda _: vmem(), outs) if out_specs is None else out_specs,
        scratch_shapes=list(scratch),
        input_output_aliases=alias or {},
        compiler_params=pltpu.CompilerParams(vmem_limit_bytes=limit),
        cost_estimate=pl.CostEstimate(flops=10**8, bytes_accessed=10**6, transcendentals=0),
    )(*args)


def shape(*dims, kind=BF16):
    return jax.ShapeDtypeStruct(dims, kind)


def place(parts):
    layer = lax.axis_index("layer")
    cores = lax.axis_size("layer") // parts
    return lax.axis_index("lat"), lax.div(layer, cores), lax.rem(layer, cores)


def xor(a, b):
    return jnp.bitwise_xor(a, b)


def lanes(index, size):
    return pl.ds(pl.multiple_of(index * size, size), size)


def wanted_tile(ids_ref, block, owner, tiles):
    found = jnp.int32(-1)
    base = owner * tiles
    for slot in range(ids_ref.shape[1]):
        tile = ids_ref[block, slot]
        here = (tile >= base) & (tile < base + tiles)
        found = jnp.where(here, tile - base, found)
    return found


def send_lanes(ids_ref, me, step, tiles):
    tile = wanted_tile(ids_ref, xor(me, step), me, tiles)
    return lanes(jnp.maximum(tile, 0), TILE)


def bias_rows(ids_ref, bias_ref, me, step):
    tiles = bias_ref.shape[0]
    tile = wanted_tile(ids_ref, xor(me, step), me, tiles)
    row = lax.broadcasted_iota(jnp.int32, bias_ref.shape, 0)
    picked = jnp.where(row == tile, bias_ref[...].astype(F32), 0.0)
    line = jnp.sum(picked, axis=0, keepdims=True)
    live = jnp.where(tile >= 0, 1.0, 0.0)
    row = lax.broadcasted_iota(jnp.int32, (EXTRA, TILE), 0)
    return jnp.where(row == 0, line, live).astype(BF16)


def pack_kernel(owners, tiles, parts, ids_in, acts_ref, enc_ref, dec_ref, bias_in, offset_in, *rest):
    count = owners - 1
    encs, decs, messages = rest[:count], rest[count : 2 * count], rest[2 * count : -6]
    bias_out, ids_ref, bias_ref, offset_ref, small_sem, sem = rest[-6:]
    small = []
    for index, pair in enumerate(
        ((ids_in, ids_ref), (bias_in, bias_ref), (offset_in, offset_ref))
    ):
        small.append(pltpu.make_async_copy(*pair, small_sem.at[index]))
    for copy in small:
        copy.start()
    features, rows = acts_ref.shape
    quarter = rows // parts
    me, part, _ = place(parts)
    inner = pl.ds(0, features)
    early = []
    for step in range(parts):
        acts = acts_ref.at[:, lanes(xor(part, step), quarter)]
        target = messages[step].at[inner, pl.ds(0, quarter)]
        early.append(pltpu.make_async_copy(acts, target, small_sem.at[3 + step]))
    for copy in early:
        copy.start()
    small[0].wait()
    pairs = []
    for step in range(1, owners):
        where = send_lanes(ids_ref, me, step, tiles)
        pairs.append((enc_ref.at[:, where], encs[step - 1]))
        pairs.append((dec_ref.at[:, where], decs[step - 1].at[inner, :]))
    here = send_lanes(ids_ref, me, 0, tiles)
    for step in range(parts):
        start = quarter
        for source in (enc_ref.at[:, here], dec_ref.at[:, here]):
            pairs.append((source, messages[step].at[inner, pl.ds(start, TILE)]))
            start += TILE
    copies = [pltpu.make_async_copy(a, b, sem.at[i]) for i, (a, b) in enumerate(pairs)]
    for copy in copies:
        copy.start()
    for copy in small[1:]:
        copy.wait()
    offset = offset_ref[...]
    high = offset.astype(BF16)
    rest_one = offset - high.astype(F32)
    middle = rest_one.astype(BF16)
    low = (rest_one - middle.astype(F32)).astype(BF16)
    row = lax.broadcasted_iota(jnp.int32, (EXTRA, features), 0)
    split = jnp.where(row == 0, high.astype(F32), 0.0)
    split = jnp.where(row == 1, middle.astype(F32), split)
    split = jnp.where(row == 2, low.astype(F32), split).astype(BF16)
    for step in range(parts):
        messages[step][pl.ds(features, EXTRA), :] = jnp.zeros((EXTRA, quarter + 2 * TILE), BF16)
        messages[step][pl.ds(features, EXTRA), pl.ds(0, features)] = split
    for step in range(1, owners):
        decs[step - 1][pl.ds(features, EXTRA), :] = bias_rows(ids_ref, bias_ref, me, step)
    bias_out[...] = bias_rows(ids_ref, bias_ref, me, 0)
    for copy in early + copies:
        copy.wait()


def join_kernel(*refs):
    out_ref = refs[-1]
    for step, ref in enumerate(refs[:-1]):
        out_ref[:, pl.ds(step * TILE, TILE)] = ref[...]


def join_bias_kernel(owners, bias_ref, *refs):
    got, out_ref, bias_out = refs[: owners - 1], refs[-2], refs[-1]
    features = out_ref.shape[0]
    bias_out[:, pl.ds(0, TILE)] = bias_ref[...]
    for step in range(owners - 1):
        out_ref[:, pl.ds(step * TILE, TILE)] = got[step][pl.ds(0, features), :]
        bias_out[:, pl.ds((step + 1) * TILE, TILE)] = got[step][pl.ds(features, EXTRA), :]


def zero_kernel(*refs):
    outs, hold, sem = refs[:-2], refs[-2], refs[-1]
    hold[...] = jnp.zeros_like(hold)
    width = hold.shape[1]
    copies = []
    for out in outs:
        for start in range(0, out.shape[1], width):
            target = out.at[:, pl.ds(start, width)]
            copies.append(pltpu.make_async_copy(hold, target, sem.at[len(copies)]))
    for copy in copies:
        copy.start()
    for copy in copies:
        copy.wait()


def preact_kernel(parts, *refs):
    messages, encs, out_ref = refs[:parts], refs[parts : 2 * parts], refs[-1]
    features = encs[0].shape[0]
    quarter = out_ref.shape[1]
    inner = pl.ds(0, features)
    one, two = None, None
    for step in range(parts):
        acts = messages[step][inner, pl.ds(0, quarter)]
        first = dot(messages[step][inner, pl.ds(quarter, TILE)], acts, 0, 0).astype(BF16).astype(F32)
        second = dot(encs[step][...], acts, 0, 0).astype(BF16).astype(F32)
        one = first if one is None else one + first
        two = second if two is None else two + second
    out_ref[pl.ds(0, TILE), :] = one
    out_ref[pl.ds(TILE, out_ref.shape[0] - TILE), :] = two


def codes_of(mine_ref, other_ref, bias_ref):
    quarter = mine_ref.shape[1]
    row = lax.broadcasted_iota(jnp.int32, (EXTRA, quarter), 0)
    bias = dot(bias_ref[...], jnp.where(row == 0, 1.0, 0.0).astype(BF16), 0, 0)
    live = dot(bias_ref[...], jnp.where(row == 1, 1.0, 0.0).astype(BF16), 0, 0)
    pre = mine_ref[...] + other_ref[...] + bias
    return (jnp.maximum(pre, 0.0) * live).astype(BF16)


def decode_kernel(count, cores, parts, scale, first, last, *refs):
    refs = list(refs)
    if first:
        sources = [refs.pop(0) for _ in range(3)]
        codes_ref = refs.pop(2 * count)
        codes_ref[...] = codes_of(*sources)
        before = None
    else:
        codes_ref, before = refs.pop(0), refs.pop(0)
    messages, decs = refs[:count], refs[count : 2 * count]
    grads = refs[2 * count : 3 * count]
    outs = refs[3 * count :]
    features, width = grads[0].shape
    quarter = codes_ref.shape[1]
    inner = pl.ds(0, features)
    row = lax.broadcasted_iota(jnp.int32, (EXTRA, quarter), 0)
    pick = jnp.where(row < 3, 1.0, 0.0).astype(BF16)
    codes = codes_ref[...]
    one = None if first else before[pl.ds(0, TILE), :]
    two = None if first else before[pl.ds(TILE, width - TILE), :]
    for step in range(count):
        message, dec = messages[step], decs[step][...]
        acts = message[inner, pl.ds(0, quarter)].astype(F32)
        tile = message[inner, pl.ds(quarter + TILE, TILE)]
        offset = dot(message[pl.ds(features, EXTRA), pl.ds(0, features)], pick, 0, 0)
        rebuilt = dot(tile, codes[:TILE], 1, 0) + dot(dec, codes[TILE:], 1, 0) + offset
        err = ((rebuilt - acts) * scale).astype(BF16)
        grads[step][...] = dot(err, codes, 1, 1).astype(BF16)
        left = dot(tile, err, 0, 0).astype(BF16).astype(F32)
        right = dot(dec, err, 0, 0).astype(BF16).astype(F32)
        one = left if one is None else one + left
        two = right if two is None else two + right
    if last:
        _, _, core = place(parts)
        half = width // cores
        hold = outs[-1]
        for block in range(cores):
            start, stop = block * half, (block + 1) * half
            if start == 0:
                hold[xor(core, block), pl.ds(0, TILE), :] = one
                hold[xor(core, block), pl.ds(TILE, half - TILE), :] = two[: half - TILE]
            else:
                hold[xor(core, block)] = two[start - TILE : stop - TILE]
        for step in range(cores):
            outs[step][...] = hold[step]
    else:
        total = outs[-1]
        total[pl.ds(0, TILE), :] = one
        total[pl.ds(TILE, width - TILE), :] = two


def mask_kernel(parts, codes_ref, *refs):
    sums, out_ref = refs[:-1], refs[-1]
    _, _, core = place(parts)
    codes = codes_ref[lanes(core, out_ref.shape[0]), :].astype(F32)
    total = sums[0][...]
    for other in sums[1:]:
        total = total + other[...]
    out_ref[...] = jnp.where(codes > 0, total, 0.0).astype(BF16)


def sum_kernel(parts, owners, *refs):
    total = None
    for step in range(parts):
        part = refs[step][...].astype(F32)
        total = part if total is None else total + part
    total = total.astype(BF16)
    for step in range(owners):
        refs[parts + step][...] = total[:, step * TILE : (step + 1) * TILE]


def encgrad_kernel(parts, cores, owners, *refs):
    acts, pieces = refs[:cores], refs[cores : cores + parts]
    outs, all_ref = refs[cores + parts : -1], refs[-1]
    quarter = pieces[0].shape[1]
    features = acts[0].shape[0]
    share = owners // cores
    _, part, _ = place(parts)
    for step in range(parts):
        all_ref[:, lanes(xor(part, step), quarter)] = pieces[step][...]
    grads = all_ref[...]
    bias = dot(jnp.ones((EXTRA, grads.shape[1]), BF16), grads, 1, 1).astype(BF16)
    for step in range(cores):
        back = dot(acts[step][...], grads, 1, 1).astype(BF16)
        for tile in range(share):
            where = slice(tile * TILE, (tile + 1) * TILE)
            outs[step * share + tile][pl.ds(0, features), :] = back[:, where]
            outs[step * share + tile][pl.ds(features, EXTRA), :] = bias[:, where]


def place_kernel(owners, cores, tiles, parts, crossed, ids_ref, zero_ref, *refs):
    got, out_ref = refs[:owners], refs[owners]
    hold, sem = refs[-2], refs[-1]
    features = out_ref.shape[0]
    me, _, core = place(parts)
    share = owners // cores
    found = []
    for step in range(owners):
        slot = xor(core, step // share) * share + step % share if crossed else step
        found.append(wanted_tile(ids_ref, xor(me, slot), me, tiles))
    if crossed:
        bias_out, bias_hold, bias_sem = refs[owners + 1], refs[-4], refs[-3]
        bias_hold[...] = jnp.zeros_like(bias_hold)
        bias_copy = pltpu.make_async_copy(bias_hold, bias_out, bias_sem)
    fresh = []
    for step in range(owners):
        new = found[step] >= 0
        for peer in range(step):
            new = new & (found[peer] != found[step])
        fresh.append(new)

    def copy(step, source):
        where = lanes(jnp.maximum(found[step], 0), TILE)
        return pltpu.make_async_copy(source, out_ref.at[:, where], sem.at[step])

    for step in range(owners):
        again = jnp.bool_(False)
        for peer in range(step + 1, owners):
            again = again | (found[peer] == found[step])

        @pl.when(fresh[step] & jnp.logical_not(again))
        def _():
            copy(step, got[step].at[pl.ds(0, features), :]).start()

        @pl.when(fresh[step] & again)
        def _():
            total = got[step][pl.ds(0, features), :].astype(F32)
            for peer in range(step + 1, owners):
                same = got[peer][pl.ds(0, features), :].astype(F32)
                total = total + jnp.where(found[peer] == found[step], same, 0.0)
            hold[step] = total.astype(BF16)
            copy(step, hold.at[step]).start()

        if crossed:

            @pl.when(fresh[step])
            def _():
                total = got[step][pl.ds(features, EXTRA), :].astype(F32)
                for peer in range(step + 1, owners):
                    same = got[peer][pl.ds(features, EXTRA), :].astype(F32)
                    total = total + jnp.where(found[peer] == found[step], same, 0.0)
                bias_hold[:, lanes(found[step], TILE)] = total[:1]

    if crossed:
        bias_copy.start()
    for step in range(owners):

        @pl.when(fresh[step])
        def _():
            copy(step, hold.at[step]).wait()

    if crossed:
        bias_copy.wait()


def sizes(mesh):
    owners, layers = mesh.shape["lat"], mesh.shape["layer"]
    parts = min(PARTS, layers)
    return owners, layers, parts, layers // parts


def local(owners, layers, parts, cores, activations, w_enc, w_dec, b_enc, b_dec, tile_ids):
    features, rows = activations.shape
    latents = w_enc.shape[1]
    tiles = latents // TILE
    width = owners * TILE
    half = width // cores
    quarter = rows // parts
    share = owners // cores

    def over_lat(x, step):
        return lax.ppermute(x, "lat", [(i, i ^ step) for i in range(owners)])

    def over_layer(x, step, stride):
        return lax.ppermute(x, "layer", [(i, i ^ (step * stride)) for i in range(layers)])

    def crossed(x, step):
        pairs = []
        for layer in range(layers):
            part, core = layer // cores, layer % cores
            goal = part * cores + (core ^ (step // share))
            for z in range(owners):
                owner = z ^ (core * share + step % share)
                pairs.append((layer * owners + z, goal * owners + owner))
        return lax.ppermute(x, ("layer", "lat"), pairs)

    def gather(x):
        return [x] + [over_layer(x, s, cores) for s in range(1, parts)]

    bias_line = b_enc.reshape(tiles, TILE)
    packed = call(
        functools.partial(pack_kernel, owners, tiles, parts),
        [shape(features, TILE)] * (owners - 1)
        + [shape(features + EXTRA, TILE)] * (owners - 1)
        + [shape(features + EXTRA, quarter + 2 * TILE)] * parts
        + [shape(EXTRA, TILE)],
        [anywhere()] * 6,
        (
            in_hbm(tile_ids),
            in_hbm(activations),
            in_hbm(w_enc),
            in_hbm(w_dec),
            in_hbm(bias_line),
            in_hbm(b_dec.reshape(1, features)),
        ),
        scratch=[
            pltpu.SMEM(tile_ids.shape, jnp.int32),
            pltpu.VMEM((tiles, TILE), BF16),
            pltpu.VMEM((1, features), F32),
            pltpu.SemaphoreType.DMA((3 + parts,)),
            pltpu.SemaphoreType.DMA((2 * parts + 2 * (owners - 1),)),
        ],
    )
    count = owners - 1
    zenc, zdec = packed[:count], packed[count : 2 * count]
    messages, own_bias = packed[2 * count : -1], packed[-1]
    zenc = [over_lat(x, s + 1) for s, x in enumerate(zenc)]
    zdec = [over_lat(x, s + 1) for s, x in enumerate(zdec)]
    messages = [messages[0]] + [over_layer(messages[s], s, cores) for s in range(1, parts)]
    all_acts = [activations] + [over_layer(activations, s, 1) for s in range(1, cores)]
    enc_rest = call(join_kernel, shape(features, width - TILE), [vmem()] * count, tuple(zenc))
    dec_rest, bias_rows = call(
        functools.partial(join_bias_kernel, owners),
        [shape(features, width - TILE), shape(EXTRA, width)],
        [vmem()] * owners,
        (own_bias, *zdec),
    )
    encs = gather(enc_rest)
    decs = gather(dec_rest)

    mine = call(
        functools.partial(preact_kernel, parts),
        shape(width, quarter, kind=F32),
        [vmem()] * (2 * parts),
        (*messages, *encs),
    )
    step = 1
    while 2 * step < cores:
        mine = mine + over_layer(mine, step, 1)
        step = 2 * step
    other = over_layer(mine, step, 1)
    groups = [list(range(parts - 1)), [parts - 1]]
    total, sent = None, []
    for index, group in enumerate(groups):
        first, last = index == 0, index == len(groups) - 1
        outs = [shape(width, quarter)] if first else []
        outs += [shape(features, width)] * len(group)
        scratch = [pltpu.VMEM((cores, half, quarter), F32)] if last else []
        if last:
            outs += [shape(half, quarter, kind=F32)] * cores
        else:
            outs += [shape(width, quarter, kind=F32)]
        args = [mine, other, bias_rows] if first else [codes, total]
        args += [messages[s] for s in group] + [decs[s] for s in group]
        out = call(
            functools.partial(
                decode_kernel, len(group), cores, parts, 1.0 / math.sqrt(rows), first, last
            ),
            outs,
            [vmem()] * len(args),
            tuple(args),
            scratch=scratch,
        )
        if first:
            codes, out = out[0], out[1:]
        sent += out[: len(group)]
        total = out[-1]
        sums = out[len(group) :]
    sums = [sums[0]] + [over_layer(sums[s], s, 1) for s in range(1, cores)]
    grad = call(
        functools.partial(mask_kernel, parts),
        shape(half, quarter),
        [vmem()] * (1 + cores),
        (codes, *sums),
    )
    grads = gather(grad)
    sent = [sent[0]] + [over_layer(sent[s], s, cores) for s in range(1, parts)]
    dec_back = call(
        functools.partial(sum_kernel, parts, owners),
        [shape(features, TILE)] * owners,
        [vmem()] * parts,
        tuple(sent),
    )
    dec_back = [dec_back[0]] + [over_lat(dec_back[s], s) for s in range(1, owners)]
    enc_back = call(
        functools.partial(encgrad_kernel, parts, cores, owners),
        [shape(features + EXTRA, TILE)] * owners,
        [vmem()] * (cores + parts),
        (*all_acts, *grads),
        scratch=[pltpu.VMEM((half, rows), BF16)],
    )
    enc_back = [crossed(x, s) for s, x in enumerate(enc_back)]
    zeros = call(
        zero_kernel,
        [shape(features, latents)] * 2,
        [],
        (),
        out_specs=[anywhere()] * 2,
        scratch=[
            pltpu.VMEM((features, 2 * TILE), BF16),
            pltpu.SemaphoreType.DMA((latents // TILE,)),
        ],
    )

    def put(cross, pieces, zero):
        outs = [shape(features, latents)] + ([shape(1, latents, kind=F32)] if cross else [])
        return call(
            functools.partial(place_kernel, owners, cores, tiles, parts, cross),
            outs,
            [smem(), anywhere()] + [vmem()] * owners,
            (in_hbm(tile_ids), zero, *pieces),
            out_specs=[anywhere()] * len(outs),
            scratch=([pltpu.VMEM((1, latents), F32), pltpu.SemaphoreType.DMA] if cross else [])
            + [pltpu.VMEM((owners, features, TILE), BF16), pltpu.SemaphoreType.DMA((owners,))],
            alias={1: 0},
        )

    (d_w_dec,) = put(False, dec_back, zeros[0])
    d_w_enc, d_b_enc = put(True, enc_back, zeros[1])
    return (d_w_enc, d_w_dec, d_b_enc.reshape(latents))


def solution(mesh):
    owners, layers, parts, cores = sizes(mesh)

    def body(*args):
        return local(owners, layers, parts, cores, *args)

    return jax.shard_map(
        body,
        mesh=mesh,
        in_specs=(
            P("layer", "lat"),
            P("layer", "lat"),
            P("layer", "lat"),
            P("lat"),
            P("layer"),
            P(),
        ),
        out_specs=(P("layer", "lat"), P("layer", "lat"), P("lat")),
        check_vma=False,
    )
```
